32 devices in a mesh: win: 2 (over y), tmpl: 4 (over z), sta: 4 (over x, core).
Axes of the slice: x: 2, y: 2, z: 4, core: 2. Of those that a mesh axis runs over, the one named last changes fastest.
Arguments:
- records: bfloat16 [384, 3, 3584], P(('win', 'sta')), parts along dimension 0
- templates: bfloat16 [16, 192, 3, 100], P(('win', 'tmpl'), 'sta'), parts along dimension 0
- channel_valid: int32 [16, 192, 3], P(('win', 'tmpl'), 'sta'), parts along dimension 0, may hold values from 0 to 1, as said below
- shifts: int32 [16, 192], P(('win', 'tmpl'), 'sta'), parts along dimension 0, may hold values from 0 to 412, as said below
- hypo_id: int32 [16], P(('win', 'tmpl')), parts along dimension 0, may hold values from 0 to 255
- hypo_xyz: float32 [3, 256], replicated, may hold values from -1 to 1
Outputs:
- peak_score: float32 [6144], P(('win', 'sta')), parts along dimension 0
- evidence: float32 [6144], P(('win', 'sta')), parts along dimension 0
- location: float32 [3, 6144], P(None, ('win', 'sta')), parts along dimension 1
The draws below stay inside these ranges and needn't reach their ends.
There are 2 independent parts, one for each index of `win`. The reference program is written for one: setup_inputs(seed, part) draws one part's arguments, and reference() takes and returns one part's arrays. A program takes and returns all parts, laid end to end along the dimension named above; an argument that names none is the same for every part. Nothing has to cross between parts.
Inputs may be any that keep to these rules, and one draw needn't show every extreme that they name: `channel_valid`: every template has all three channels of at least one station valid. `shifts`: for every template some station has moveout 0.
All inputs are finite; a program needn't handle non-finite values.
Results may differ from the reference program's by a relative error of at most 0.0044.
Values sent between devices are 32-bit elements; how exact they have to be, the bound alone decides.
No kernel may reach another device: no remote copies, remote signals or barrier semaphores. Data moves between devices by JAX's collectives and lax.ppermute only.
A program may use at most 64 MiB of HBM per device.

```python
import math
import jax
import jax.numpy as jnp
from jax import lax

STATIONS = 192
TAPS = 100
PAD = 512
HYPOS = 256
TMPL_DEV = 2
SAMPLES = 3072
TEMPLATES = 8
RECORD = 3584


def draw_shifts(key, part):
    base = jax.random.randint(jax.random.fold_in(key, 11), (TEMPLATES, STATIONS), 0, PAD - TAPS + 1)
    row_index = jnp.arange(TEMPLATES)[:, None]
    col_index = jnp.arange(STATIONS)[None, :]
    farthest = col_index == row_index * 7 % STATIONS
    nearest = col_index == (row_index * 7 + 1) % STATIONS
    return jnp.where(farthest, PAD - TAPS, jnp.where(nearest, 0, base)).astype(jnp.int32)


def template_shapes(key):
    wave_key = jax.random.fold_in(key, 21)
    amp_key = jax.random.fold_in(key, 22)
    wave = jax.random.normal(wave_key, (TEMPLATES, STATIONS, 3, TAPS), jnp.float32)
    amplitude = jnp.exp(jax.random.uniform(amp_key, (TEMPLATES, STATIONS, 3, 1), jnp.float32, 0.0, 2.3026))
    return wave * amplitude


def draw_templates(key, part):
    return template_shapes(key).astype(jnp.bfloat16)


def draw_channel_valid(key, part):
    tickets = jax.random.randint(jax.random.fold_in(key, 31), (TEMPLATES, STATIONS, 3), 0, 1000)
    limits = 150 + 800 * jnp.arange(STATIONS) // STATIONS
    homes = jax.random.randint(jax.random.fold_in(key, 32), (TEMPLATES, 1), 0, STATIONS)
    at_home = (jnp.arange(STATIONS)[None, :] == homes)[:, :, None]
    chosen = (tickets < limits[None, :, None]) | at_home
    return chosen.astype(jnp.int32)


def draw_records(key, part):
    noise = jax.random.truncated_normal(jax.random.fold_in(key, 51), -4.0, 4.0, (STATIONS, 3, RECORD), jnp.float32)
    gains = jnp.exp(jax.random.uniform(jax.random.fold_in(key, 52), (STATIONS, 3, 1), jnp.float32, 0.0, 2.3026))
    envelope_blocks = jnp.exp(jax.random.uniform(jax.random.fold_in(key, 53), (STATIONS, 1, RECORD // 64 + 1), jnp.float32, 0.0, 1.3863))
    envelope = envelope_blocks[:, :, jnp.arange(RECORD) // 64]
    traces = noise * gains * envelope
    return traces.astype(jnp.bfloat16)


def plant(array, key, smallest, high):
    longest = array.shape.index(max(array.shape))
    spots = []
    for shift in (0, 1):
        where = [jax.random.randint(jax.random.fold_in(key, axis), (), 0, length) for axis, length in enumerate(array.shape)]
        where[longest] = (where[longest] + shift) % array.shape[longest]
        spots.append(tuple(where))
    return array.at[spots[0]].set(smallest).at[spots[1]].set(high)


def setup_inputs(seed: int = 0, part: int = 0) -> dict:
    key_list = jax.random.split(jax.random.key(seed), 7)
    own_keys = jax.random.split(jax.random.fold_in(key_list[6], part), 7)
    records = draw_records(jax.random.fold_in(jax.random.fold_in(key_list[6], part), 71), part)
    templates = draw_templates(jax.random.fold_in(jax.random.fold_in(key_list[6], part), 71), part)
    channel_valid = draw_channel_valid(jax.random.fold_in(jax.random.fold_in(key_list[6], part), 71), part)
    shifts = draw_shifts(jax.random.fold_in(jax.random.fold_in(key_list[6], part), 71), part)
    hypo_id = plant(jax.random.randint(own_keys[4], (TEMPLATES,), 0, HYPOS), jax.random.fold_in(own_keys[4], 1), 0, HYPOS - 1).astype(jnp.int32)
    hypo_xyz = jnp.clip(jax.random.uniform(key_list[5], (3, HYPOS), jnp.float32, -1.0, 1.0), -1.0, 1.0)
    return dict(records=records, templates=templates, channel_valid=channel_valid, shifts=shifts, hypo_id=hypo_id, hypo_xyz=hypo_xyz)


sharpness = 400.0
epsilon = 1e-06

def normed_templates(templates):
    wide = templates.astype(jnp.float32)
    power = lax.optimization_barrier(jnp.mean(wide * wide, axis=-1, keepdims=True))
    return (wide / (wide.shape[-1] * jnp.sqrt(power + epsilon))).astype(jnp.bfloat16)

def window_norm(channels, taps_len):
    squares = channels.astype(jnp.float32) * channels.astype(jnp.float32)
    ones_kernel = jnp.ones((squares.shape[0], 1, taps_len), jnp.float32)
    energy = lax.conv_general_dilated(squares[None], ones_kernel, (1,), 'VALID', dimension_numbers=('NCH', 'OIH', 'NCH'), feature_group_count=squares.shape[0], precision=lax.Precision.HIGHEST)[0]
    return jnp.sqrt(energy / taps_len + epsilon)

def block_trace(records_blk, normed_blk, valid_blk, shift_blk, out_length):
    sta_count, comp_count, in_length = records_blk.shape
    tpl_count, taps_len = (normed_blk.shape[0], normed_blk.shape[-1])
    chan_count = sta_count * comp_count
    channels = records_blk.reshape(chan_count, in_length)
    kernel = jnp.transpose(normed_blk, (1, 2, 0, 3)).reshape(chan_count * tpl_count, 1, taps_len)
    raw_corr = lax.conv_general_dilated(channels[None], kernel, (1,), 'VALID', dimension_numbers=('NCH', 'OIH', 'NCH'), feature_group_count=chan_count, preferred_element_type=jnp.float32)[0]
    norms = window_norm(channels, taps_len)
    weights = jnp.transpose(valid_blk, (1, 2, 0)).reshape(chan_count, tpl_count).astype(jnp.float32)
    scaled = raw_corr.reshape(chan_count, tpl_count, -1) / norms[:, None, :] * weights[:, :, None]
    station_sum = lax.optimization_barrier(jnp.sum(scaled.reshape(sta_count, comp_count, tpl_count, -1), axis=1))

    def align(row, offset):
        return lax.dynamic_slice_in_dim(row, offset.astype(jnp.int32), out_length)
    aligned = jax.vmap(jax.vmap(align))(station_sum, shift_blk.T)
    return lax.optimization_barrier(jnp.sum(aligned, axis=0))

def correlate(records, normed, channel_valid, shifts, out_length):
    sta_total = records.shape[0]
    block_size = math.gcd(sta_total, 8)

    def accumulate(totals, block_index):
        first_row = (block_index * block_size).astype(jnp.int32)
        part_records = lax.dynamic_slice_in_dim(records, first_row, block_size, 0)
        part_normed = lax.dynamic_slice_in_dim(normed, first_row, block_size, 1)
        part_valid = lax.dynamic_slice_in_dim(channel_valid, first_row, block_size, 1)
        part_shift = lax.dynamic_slice_in_dim(shifts, first_row, block_size, 1)
        return (totals + block_trace(part_records, part_normed, part_valid, part_shift, out_length), None)
    start_value = jnp.zeros((normed.shape[0], out_length), jnp.float32)
    totals, unused = lax.scan(accumulate, start_value, jnp.arange(sta_total // block_size, dtype=jnp.int32))
    return totals

def reference(records, templates, channel_valid, shifts, hypo_id, hypo_xyz):
    normed = normed_templates(templates)

    def per_block(block_index):
        first_tpl = (block_index * TMPL_DEV).astype(jnp.int32)
        block_normed = lax.dynamic_slice_in_dim(normed, first_tpl, TMPL_DEV, 0)
        block_valid = lax.dynamic_slice_in_dim(channel_valid, first_tpl, TMPL_DEV, 0)
        block_shift = lax.dynamic_slice_in_dim(shifts, first_tpl, TMPL_DEV, 0)
        return correlate(records, block_normed, block_valid, block_shift, SAMPLES)
    traces = lax.map(per_block, jnp.arange(TEMPLATES // TMPL_DEV, dtype=jnp.int32)).reshape(TEMPLATES, SAMPLES)
    counts = lax.optimization_barrier(jnp.sum(channel_valid, axis=(1, 2))).astype(jnp.float32)
    scores = sharpness * (traces / counts[:, None])
    peak_score = lax.optimization_barrier(jnp.max(scores, axis=0))
    weights = jnp.exp(scores - peak_score[None, :])
    totals = lax.optimization_barrier(jnp.sum(weights, axis=0))
    evidence = peak_score + jnp.log(totals)
    positions = hypo_xyz[:, hypo_id]
    located = jnp.dot(positions, weights, precision=lax.Precision.HIGHEST)
    location = located / totals[None, :]
    return (peak_score, evidence, location)
```

```python
import functools
import jax, jax.numpy as jnp
from jax import lax
from jax.experimental import pallas as pl
from jax.experimental.pallas import tpu as pltpu

from jax.sharding import PartitionSpec as P

SAMPLES = 3072
LANES = 128
sharpness = 400.0
epsilon = 1e-06
BIG = 3.0e38

def trace_kernel(group, out_rows, shares, copies, shift_ref, valid_ref, id_ref, rec_ref, tmpl_ref, xyz_ref,
                 out_ref, wav, rows, inv, slot):
    tpls, stas, comps, taps = tmpl_ref.shape
    blocks = rec_ref.shape[-1] // LANES
    pitch = rows.shape[0] // (stas * comps)
    f32 = jnp.float32
    lane = lax.broadcasted_iota(jnp.int32, (LANES, LANES), 1)
    sub = lax.broadcasted_iota(jnp.int32, (LANES, LANES), 0)
    same = lane >= sub

    wav[...] = jnp.zeros(wav.shape, f32)
    for t in range(tpls):
        wide = tmpl_ref[t].astype(f32)
        power = jnp.mean(wide * wide, axis=-1, keepdims=True)
        normed = (wide / (taps * jnp.sqrt(power + epsilon))).astype(jnp.bfloat16).astype(f32)
        wav[t, :, :comps, :taps] = normed

    def spread(s, _):
        wide = rec_ref[s].astype(f32)
        base = s * (comps * pitch)
        for q in range(blocks):
            rows[pl.ds(base + q, comps, stride=pitch), :] = wide[:, q * LANES:(q + 1) * LANES]
        for c in range(comps):
            rows[pl.ds(base + c * pitch + blocks, pitch - blocks), :] = jnp.zeros((pitch - blocks, LANES), f32)
        return _
    lax.fori_loop(0, stas, spread, 0)

    near = (lane < sub + taps) & same
    far = (lane + LANES < sub + taps)
    band = jnp.concatenate([jnp.concatenate([near.astype(f32)] * 2, axis=1),
                            jnp.concatenate([far.astype(f32)] * 2, axis=1)], axis=0).astype(jnp.bfloat16)
    chans = group * comps
    chunk = chans * pitch

    def energy(g, _):
        base = pl.multiple_of(g * chunk, 8)
        wide = rows[pl.ds(base, chunk), :]
        square = jnp.minimum(wide * wide, BIG)
        high = square.astype(jnp.bfloat16)
        low = (square - high.astype(f32)).astype(jnp.bfloat16)
        both = lax.dot_general(jnp.concatenate([high, low], axis=1), band,
                               (((1,), (1,)), ((), ())), preferred_element_type=f32)
        nxt = pltpu.roll(both[:, LANES:], chunk - 1, axis=0)
        inv[pl.ds(base, chunk), :] = lax.rsqrt((both[:, :LANES] + nxt) / taps + epsilon)
        return _
    lax.fori_loop(0, stas // group, energy, 0)

    row_lane = lax.broadcasted_iota(jnp.int32, (out_rows, LANES), 1)

    def step(g, carry):
        accs, counts = list(carry[0]), list(carry[1])
        for u in range(group):
            s = g * group + u
            parts = [None] * tpls
            for c in range(comps):
                base = pl.multiple_of((s * comps + c) * pitch, 8)
                here = rows[pl.ds(base, pitch), :].astype(jnp.bfloat16)
                there = rows[pl.ds(base + 1, pitch), :].astype(jnp.bfloat16)
                left = jnp.concatenate([here, there], axis=1)
                bands = []
                for t in range(tpls):
                    used = valid_ref[t, s, c]
                    counts[t] = counts[t] + used
                    wave = wav[t, s, pl.ds(c, 1), :] * used.astype(f32)
                    ring = pltpu.roll(jnp.broadcast_to(wave, (LANES, LANES)), 0, 1, stride=1, stride_axis=0)
                    bands.append(jnp.concatenate([jnp.where(same, ring, 0.0).astype(jnp.bfloat16),
                                                  jnp.where(same, 0.0, ring).astype(jnp.bfloat16)], axis=1))
                raw = lax.dot_general(left, jnp.concatenate(bands, axis=0), (((1,), (1,)), ((), ())),
                                      preferred_element_type=f32)
                scale = inv[pl.ds(base, pitch), :]
                for t in range(tpls):
                    term = raw[:, t * LANES:(t + 1) * LANES] * scale
                    parts[t] = term if c == 0 else parts[t] + term
            for t in range(tpls):
                shift = shift_ref[t, s]
                skip, turn = shift // LANES, lax.rem(shift, LANES)
                slot[u * tpls + t] = pltpu.roll(parts[t], lax.rem(LANES - turn, LANES), 1)
                first = slot[u * tpls + t, pl.ds(skip, out_rows), :]
                second = slot[u * tpls + t, pl.ds(skip + 1, out_rows), :]
                accs[t] = accs[t] + jnp.where(row_lane < LANES - turn, first, second)
        return tuple(accs), tuple(counts)

    zero = (tuple(jnp.zeros((out_rows, LANES), f32) for _ in range(tpls)), tuple(jnp.int32(0) for _ in range(tpls)))
    accs, counts = lax.fori_loop(0, stas // group, step, zero)

    share = out_rows // shares
    place = lax.broadcasted_iota(jnp.int32, xyz_ref.shape, 1)
    diag = lax.broadcasted_iota(jnp.int32, (xyz_ref.shape[0], LANES), 0) == lax.broadcasted_iota(
        jnp.int32, (xyz_ref.shape[0], LANES), 1)
    for t in range(tpls):
        spot = jnp.sum(jnp.where(place == id_ref[t], xyz_ref[...], 0.0), axis=1, keepdims=True)
        where = jnp.sum(jnp.where(diag, spot, 0.0), axis=0, keepdims=True)
        count = jnp.full((1, LANES), counts[t].astype(f32), f32)
        for b in range(shares):
            for d in range(copies):
                out_ref[d * shares + b, pl.ds(t * share, share), :] = accs[t][b * share:(b + 1) * share]
                out_ref[d * shares + b, pl.ds(tpls * share + t, 1), :] = count
                out_ref[d * shares + b, pl.ds(tpls * share + tpls + t, 1), :] = where


def block_rows(tpls, out_rows, shares):
    need = tpls * (out_rows // shares) + 2 * tpls
    return -(-need // 8) * 8

def traces_call(records, templates, valid, shifts, ids, xyz, out_rows, shares, copies, group=4, interpret=False):
    tpls, stas, comps, taps = templates.shape
    while stas % group: group -= 1
    blocks = records.shape[-1] // LANES
    pitch = -(-(blocks + 1) // 8) * 8
    smem = pl.BlockSpec(memory_space=pltpu.SMEM)
    vmem = pl.BlockSpec(memory_space=pltpu.VMEM)
    return pl.pallas_call(
        functools.partial(trace_kernel, group, out_rows, shares, copies),
        out_shape=jax.ShapeDtypeStruct((copies * shares, block_rows(tpls, out_rows, shares), LANES), jnp.float32),
        in_specs=[smem, smem, smem, vmem, vmem, vmem],
        out_specs=vmem,
        scratch_shapes=[
            pltpu.VMEM((tpls, stas, 8, LANES), jnp.float32),
            pltpu.VMEM((stas * comps * pitch + 8, LANES), jnp.float32),
            pltpu.VMEM((stas * comps * pitch, LANES), jnp.float32),
            pltpu.VMEM((group * tpls, pitch, LANES), jnp.float32),
        ],
        name="traces",
        interpret=interpret,
    )(shifts, valid, ids, records, templates, xyz)


def merge_kernel(shares, tpls, got_ref, peak_ref, evidence_ref, place_ref):
    groups = got_ref.shape[0] // shares
    share = peak_ref.shape[0]
    scores, spots = [], []
    for g in range(groups):
        total = got_ref[g * shares]
        for s in range(1, shares):
            total = total + got_ref[g * shares + s]
        for t in range(tpls):
            trace = total[t * share:(t + 1) * share]
            count = total[tpls * share + t:tpls * share + t + 1]
            scores.append(sharpness * (trace / count))
            row = tpls * share + tpls + t
            spots.append(got_ref[g * shares, row:row + 1, :])
    peak = functools.reduce(jnp.maximum, scores)
    weights = [jnp.exp(score - peak) for score in scores]
    totals = functools.reduce(jnp.add, weights)
    peak_ref[...] = peak
    evidence_ref[...] = peak + jnp.log(totals)
    for j in range(place_ref.shape[0]):
        located = functools.reduce(jnp.add, [w * spot[:, j:j + 1] for w, spot in zip(weights, spots)])
        located = located / totals
        for q in range(share):
            place_ref[j:j + 1, q * LANES:(q + 1) * LANES] = located[q:q + 1]


def on_device(records, templates, channel_valid, shifts, hypo_id, hypo_xyz):
    shares, copies = lax.axis_size("sta"), lax.axis_size("tmpl")
    tpls = templates.shape[0]
    share = SAMPLES // LANES // shares
    sent = traces_call(records, templates, channel_valid, shifts, hypo_id, hypo_xyz, SAMPLES // LANES, shares, copies)
    got = lax.all_to_all(sent, ("tmpl", "sta"), 0, 0, tiled=True)
    flat = jax.ShapeDtypeStruct((share, LANES), jnp.float32)
    vmem = pl.BlockSpec(memory_space=pltpu.VMEM)
    peak, evidence, location = pl.pallas_call(
        functools.partial(merge_kernel, shares, tpls),
        out_shape=(flat, flat, jax.ShapeDtypeStruct((hypo_xyz.shape[0], share * LANES), jnp.float32)),
        in_specs=[vmem],
        out_specs=(vmem, vmem, vmem),
        name="merge",
    )(got)
    return peak.reshape(-1), evidence.reshape(-1), location


def solution(mesh):
    return jax.shard_map(
        on_device,
        mesh=mesh,
        in_specs=(
            P(("win", "sta"), None, None),
            P(("win", "tmpl"), "sta", None, None),
            P(("win", "tmpl"), "sta", None),
            P(("win", "tmpl"), "sta"),
            P(("win", "tmpl")),
            P(),
        ),
        out_specs=(P(("win", "sta")), P(("win", "sta")), P(None, ("win", "sta"))),
        check_vma=False,
    )
```
